512 devices in a mesh: segment: 4 (over z_hi, core), expert: 128 (over y, x, z_lo).
Axes of the slice: x: 4, y: 4, z: 16 (z_hi: 2, z_lo: 8; z = z_hi * 8 + z_lo), core: 2. Of those that a mesh axis runs over, the one named last changes fastest.
Arguments:
- fwd_input: bfloat16 [4, 8192, 1024], P('segment', 'expert'), may hold values from -6 to 6
- fwd_routes: int32 [4, 8192, 8], P('segment', 'expert'), may hold values from 0 to 127, all different within a row; in each aligned block of 64 rows (0 to 63, 64 to 127, ..., all dimensions but the last counted through in order) at most 4 rows name the same one
- fwd_gates: float32 [4, 8192, 8], P('segment', 'expert'), may hold values from 0.05 to 0.3
- bwd_input: bfloat16 [4, 8192, 1024], P('segment', 'expert'), may hold values from -6 to 6
- bwd_grad: bfloat16 [4, 8192, 1024], P('segment', 'expert'), may hold values from -6 to 6
- bwd_routes: int32 [4, 8192, 8], P('segment', 'expert'), may hold values from 0 to 127, all different within a row; in each aligned block of 64 rows (0 to 63, 64 to 127, ..., all dimensions but the last counted through in order) at most 4 rows name the same one
- bwd_gates: float32 [4, 8192, 8], P('segment', 'expert'), may hold values from 0.05 to 0.3
- norm_gain: float32 [4, 1024], P('segment'), may hold values from 0.25 to 1.75
- w_gate: bfloat16 [4, 128, 1024, 768], P('segment', 'expert'), may hold values from -0.1875 to 0.1875
- w_up: bfloat16 [4, 128, 1024, 768], P('segment', 'expert'), may hold values from -0.1875 to 0.1875
- w_down: bfloat16 [4, 128, 768, 1024], P('segment', 'expert'), may hold values from -0.21875 to 0.21875
Outputs:
- fwd_out: bfloat16 [4, 8192, 1024], P('segment', 'expert')
- bwd_out: bfloat16 [4, 8192, 1024], P('segment', 'expert')
The draws below stay inside these ranges and needn't reach their ends.
Inputs may be any that keep to these rules, and one draw needn't show every extreme that they name: `fwd_routes`: each token names 8 different experts; within the 64 rows of one device (aligned blocks) no expert is named by more than 4 rows, a bound that some block reaches. `bwd_routes`: as for fwd_routes.
All inputs are finite; a program needn't handle non-finite values.
Results may differ from the reference program's by a relative error of at most 0.0051.
Values may be sent and summed in bfloat16 or wider, within the bound.
A program may use at most 64 MiB of HBM per device.

```python
import math
import jax
import jax.numpy as jnp
import numpy as np
from jax import lax

D = 1024
FF = 768
TOP = 8
TOK_DEV = 64
EXPERTS = 128
LAYERS = 4
CAP = 4
TOKENS = 8192
N_EXPERT = 128


def shard_levels(own_key, shape, split, smallest, top_value):
    factor_of = 1.0
    for dim, shards_of in split:
        heights = jax.random.uniform(jax.random.fold_in(jax.random.fold_in(own_key, 6), dim), (shards_of,), jnp.float32, smallest / len(split), top_value / len(split))
        factor_of = factor_of * jnp.repeat(jnp.exp(heights), shape[dim] // shards_of).reshape((-1,) + (1,) * (len(shape) - 1 - dim))
    return factor_of


def assign_block(key, own, number, rows, amount, top, bound, slope):
    ranking = jax.random.permutation(key, amount)
    crowded, common = portions_of(amount, rows * top, bound, slope, True), portions_of(amount, rows * top, bound, slope, False)
    places = jnp.arange(amount)

    def named(sizes, offset_by):
        used = int((sizes > 0).sum())
        fixed = max(1, used // 4)
        shifted = fixed + (places - fixed + offset_by * (used - fixed)) % max(1, amount - fixed)
        return jnp.zeros((amount,), jnp.int32).at[ranking[jnp.where(places < fixed, places, shifted)]].set(jnp.asarray(sizes, jnp.int32))

    sizes = jnp.where(number % 4 == 0, named(crowded, number // 4), named(common, number - number // 4 - 1))
    mixed = jax.random.permutation(jax.random.fold_in(own, 3), amount)
    donor, taker = mixed[0:amount // 2 * 2:2], mixed[1:amount // 2 * 2:2]
    margin = jnp.minimum(sizes[donor] - 1, bound - sizes[taker]) // 2
    margin = jnp.where((donor == ranking[0]) | (taker == ranking[0]) | (sizes[taker] == 0), 0, jnp.maximum(margin, 0))
    shifted = jax.random.randint(jax.random.fold_in(own, 4), (amount // 2,), 0, 1 << 20) % (margin + 1)
    sizes = sizes.at[donor].add(-shifted).at[taker].add(shifted)
    labels = jnp.searchsorted(jnp.cumsum(sizes), jnp.arange(rows * top), side="right").astype(jnp.int32)
    table = labels.reshape(top, rows).T
    table = table[jax.random.permutation(jax.random.fold_in(own, 1), rows)]
    offset_by = jax.random.randint(jax.random.fold_in(own, 2), (rows, 1), 0, top)
    return jnp.take_along_axis(table, (jnp.arange(top)[None, :] + offset_by) % top, axis=1)


def portions_of(number_of, total, limit, skew, full):
    loads = [(1 << 20) // math.isqrt(rank ** skew) + 1 for rank in range(1, number_of + 1)]
    largest = limit if full else min(limit, max(-(-total // number_of), total * loads[0] // sum(loads)))
    least = 1 if total - largest >= number_of - 1 else 0
    given, surplus = [largest] + [least] * (number_of - 1), total - largest - least * (number_of - 1)
    while surplus > 0:
        movable = [i for i in range(1, number_of) if given[i] < largest] or [i for i in range(1, number_of) if given[i] < limit]
        whole, budget = sum([loads[i] for i in movable]), surplus
        for i in movable:
            extra = min(limit - given[i], max(1, budget * loads[i] // whole), surplus)
            given[i] = given[i] + extra
            surplus = surplus - extra
    return np.array(given)


def gaussian(key, shape, deviation, most, shards=(), kind=jnp.bfloat16):
    level = shard_levels(key, shape, shards, -0.22, 0.18) if shards else 1.0
    drawn = jax.random.normal(key, shape, jnp.float32) * deviation * level
    return jnp.minimum(jnp.maximum(drawn, -most), most).astype(kind)


def setup_inputs(seed: int = 0) -> dict:
    splits = jax.random.split(jax.random.key(seed), 12)
    fwd_input = gaussian(splits[0], (LAYERS, TOKENS, D), 1.0, 6.0, ((0, 4), (1, 128)))
    fwd_routes_keys = jax.random.split(jax.random.fold_in(splits[1], 1), LAYERS * TOKENS // TOK_DEV)
    fwd_routes_turns = jax.random.permutation(jax.random.fold_in(splits[1], 3), LAYERS * TOKENS // TOK_DEV)
    fwd_routes = jax.vmap(lambda own, number: assign_block(jax.random.fold_in(splits[1], 2), own, number, TOK_DEV, EXPERTS, TOP, CAP, 0))(fwd_routes_keys, fwd_routes_turns).reshape((LAYERS, TOKENS, TOP))
    fwd_gates = jnp.clip(0.05 + 0.25 * jax.random.uniform(splits[2], (LAYERS, TOKENS, TOP), jnp.float32) ** shard_levels(splits[2], (LAYERS, TOKENS, TOP), ((0, 4), (1, 128)), -0.2, 0.2), 0.05, 0.3)
    bwd_input = gaussian(splits[3], (LAYERS, TOKENS, D), 1.0, 6.0, ((0, 4), (1, 128)))
    bwd_grad = gaussian(splits[4], (LAYERS, TOKENS, D), 1.0, 6.0, ((0, 4), (1, 128)))
    bwd_routes_keys = jax.random.split(jax.random.fold_in(splits[5], 1), LAYERS * TOKENS // TOK_DEV)
    bwd_routes_turns = jax.random.permutation(jax.random.fold_in(splits[5], 3), LAYERS * TOKENS // TOK_DEV)
    bwd_routes = jax.vmap(lambda own, number: assign_block(jax.random.fold_in(splits[5], 2), own, number, TOK_DEV, EXPERTS, TOP, CAP, 0))(bwd_routes_keys, bwd_routes_turns).reshape((LAYERS, TOKENS, TOP))
    bwd_gates = jnp.clip(0.05 + 0.25 * jax.random.uniform(splits[6], (LAYERS, TOKENS, TOP), jnp.float32) ** shard_levels(splits[6], (LAYERS, TOKENS, TOP), ((0, 4), (1, 128)), -0.2, 0.2), 0.05, 0.3)
    norm_gain = jnp.clip(1.0 + 0.15 * jax.random.normal(splits[7], (LAYERS, D), jnp.float32), 0.25, 1.75)
    w_gate = gaussian(splits[8], (LAYERS, EXPERTS, D, FF), D ** -0.5, 0.1875, ((0, 4), (1, 128)))
    w_up = gaussian(splits[9], (LAYERS, EXPERTS, D, FF), D ** -0.5, 0.1875, ((0, 4), (1, 128)))
    w_down = gaussian(splits[10], (LAYERS, EXPERTS, FF, D), FF ** -0.5, 0.21875, ((0, 4), (1, 128)))
    return {"fwd_input": fwd_input, "fwd_routes": fwd_routes, "fwd_gates": fwd_gates, "bwd_input": bwd_input, "bwd_grad": bwd_grad, "bwd_routes": bwd_routes, "bwd_gates": bwd_gates, "norm_gain": norm_gain, "w_gate": w_gate, "w_up": w_up, "w_down": w_down}


EPSILON = 1e-06

def norm_scale(stream):
    return lax.rsqrt(lax.optimization_barrier(jnp.mean(stream * stream, axis=-1, keepdims=True)) + EPSILON)

def slot_index(routes):
    blocks = routes.reshape(N_EXPERT, TOK_DEV * TOP)
    onehot = (blocks[:, :, None] == jnp.arange(EXPERTS, dtype=jnp.int32)[None, None, :]).astype(jnp.int32)
    before = jnp.cumsum(onehot, axis=1) - onehot
    position = lax.optimization_barrier(jnp.sum(before * onehot, axis=2)).astype(jnp.int32)
    source = jnp.arange(N_EXPERT, dtype=jnp.int32)[:, None]
    return (blocks * (N_EXPERT * CAP) + source * CAP + position).reshape(-1).astype(jnp.int32)

def expert_forward(inputs, gate_matrix, up_matrix, down_matrix):
    gate = jnp.dot(inputs, gate_matrix, preferred_element_type=jnp.float32)
    upward = jnp.dot(inputs, up_matrix, preferred_element_type=jnp.float32)
    hidden = (gate * jax.nn.sigmoid(gate) * upward).astype(jnp.bfloat16)
    return jnp.dot(hidden, down_matrix, preferred_element_type=jnp.float32).astype(jnp.bfloat16)

def transposed(left, right):
    return lax.dot_general(left, right, (((1,), (1,)), ((), ())), preferred_element_type=jnp.float32)

def expert_backward(inputs, grads, gate_matrix, up_matrix, down_matrix):
    gate = jnp.dot(inputs, gate_matrix, preferred_element_type=jnp.float32)
    upward = jnp.dot(inputs, up_matrix, preferred_element_type=jnp.float32)
    d_hidden = transposed(grads, down_matrix)
    sigma = jax.nn.sigmoid(gate)
    d_gate = (d_hidden * upward * sigma * (1.0 + gate * (1.0 - sigma))).astype(jnp.bfloat16)
    d_up = (d_hidden * gate * sigma).astype(jnp.bfloat16)
    return (transposed(d_gate, gate_matrix) + transposed(d_up, up_matrix)).astype(jnp.bfloat16)

def to_buffer(values, target):
    buffer = jnp.zeros((EXPERTS * N_EXPERT * CAP, D), values.dtype).at[target].set(values)
    return buffer.reshape(EXPERTS, N_EXPERT * CAP, D)

def layer_forward(inputs, routes, gates, gain, w_gate, w_up, w_down):
    stream = inputs.astype(jnp.float32)
    normed = (stream * norm_scale(stream) * gain).astype(jnp.bfloat16)
    target = slot_index(routes)
    buffer = to_buffer(jnp.repeat(normed, TOP, axis=0), target)
    results = lax.map(lambda pack: expert_forward(*pack), (buffer, w_gate, w_up, w_down))
    picked = results.reshape(-1, D)[target].reshape(TOKENS, TOP, D).astype(jnp.float32)
    return (stream + lax.optimization_barrier(jnp.sum(gates[:, :, None] * picked, axis=1))).astype(jnp.bfloat16)

def layer_backward(inputs, grad, routes, gates, gain, w_gate, w_up, w_down):
    stream = inputs.astype(jnp.float32)
    scale = norm_scale(stream)
    normed = (stream * scale * gain).astype(jnp.bfloat16)
    grad_stream = grad.astype(jnp.float32)
    scaled = (gates[:, :, None] * grad_stream[:, None, :]).astype(jnp.bfloat16).reshape(-1, D)
    target = slot_index(routes)
    row_buffer = to_buffer(jnp.repeat(normed, TOP, axis=0), target)
    grad_buffer = to_buffer(scaled, target)
    results = lax.map(lambda pack: expert_backward(*pack), (row_buffer, grad_buffer, w_gate, w_up, w_down))
    picked = results.reshape(-1, D)[target].reshape(TOKENS, TOP, D).astype(jnp.float32)
    summed = gain * lax.optimization_barrier(jnp.sum(picked, axis=1))
    inner = lax.optimization_barrier(jnp.mean(summed * stream, axis=-1, keepdims=True))
    return (grad_stream + scale * summed - stream * scale * scale * scale * inner).astype(jnp.bfloat16)

def reference(fwd_input, fwd_routes, fwd_gates, bwd_input, bwd_grad, bwd_routes, bwd_gates, norm_gain, w_gate, w_up, w_down):
    outputs = []
    gradients = []
    for layer in range(LAYERS):
        outputs.append(layer_forward(fwd_input[layer], fwd_routes[layer], fwd_gates[layer], norm_gain[layer], w_gate[layer], w_up[layer], w_down[layer]))
        gradients.append(layer_backward(bwd_input[layer], bwd_grad[layer], bwd_routes[layer], bwd_gates[layer], norm_gain[layer], w_gate[layer], w_up[layer], w_down[layer]))
    fwd_out = jnp.roll(jnp.stack(outputs), 1, axis=0)
    bwd_out = jnp.roll(jnp.stack(gradients), -1, axis=0)
    return (fwd_out, bwd_out)
```

```python
import functools
import types

import jax
import jax.numpy as jnp
from jax import lax
from jax.experimental import pallas as pl
from jax.experimental.pallas import tpu as pltpu
from jax.sharding import PartitionSpec as P

EPSILON = 1e-06
MESH = pl.DeviceIdType.MESH
F32 = jnp.float32
BF16 = jnp.bfloat16
LINE = 8
HALVES = 2


def geometry(experts, tokens, top, width, hidden, line):
    g = types.SimpleNamespace()
    g.line = line
    g.plane = experts // line
    g.tokens = tokens
    g.top = top
    g.width = width
    g.hidden = hidden
    g.capacity = tokens * top // experts
    g.sources = line // 2
    g.rows = g.sources * g.capacity
    g.group = g.sources * tokens
    g.chunk = tokens // HALVES
    assert g.plane * g.rows == g.group
    return g


def transposed(left, right):
    return lax.dot_general(left, right, (((1,), (1,)), ((), ())), preferred_element_type=F32)


def picked_back(picks, rows):
    return lax.dot_general(picks, rows, (((0,), (0,)), ((), ())), preferred_element_type=F32)


def kernel(
    g,
    meta_in,
    gain_ref,
    fwd_in,
    bwd_in,
    grad_in,
    gate_hbm,
    up_hbm,
    down_hbm,
    y_ref,
    dx_ref,
    tok,
    meta,
    w_gate,
    w_up,
    w_down,
    picks,
    weighted,
    send,
    recv,
    made,
    back,
    part,
    acc,
    stage,
    load_sem,
    tok_send,
    tok_recv,
    meta_send,
    meta_recv,
    out_send,
    out_recv,
    own_sem,
    sum_send,
    sum_recv,
):
    me = lax.axis_index("expert")
    z = lax.rem(me, g.line)
    here = me // g.line
    half = z // g.sources
    last = g.line - 1

    def expert_at(plane, layer):
        return {"expert": plane * g.line + layer}

    def base_of(group):
        return lax.rem(half + group, 2) * g.sources

    loads = [
        pltpu.make_async_copy(meta_in, meta.at[z], load_sem.at[0]),
        pltpu.make_async_copy(fwd_in, tok.at[0, z], load_sem.at[1]),
        pltpu.make_async_copy(bwd_in, tok.at[1, z], load_sem.at[2]),
        pltpu.make_async_copy(grad_in, tok.at[2, z], load_sem.at[3]),
    ]
    weights = [
        pltpu.make_async_copy(gate_hbm, w_gate, load_sem.at[4]),
        pltpu.make_async_copy(up_hbm, w_up, load_sem.at[5]),
        pltpu.make_async_copy(down_hbm, w_down, load_sem.at[6]),
    ]
    for copy in loads + weights:
        copy.start()

    barrier = pltpu.get_barrier_semaphore()

    @pl.when(z > 0)
    def _():
        pl.semaphore_signal(barrier, inc=1, device_id=expert_at(here, z - 1), device_id_type=MESH)

    @pl.when(z < last)
    def _():
        pl.semaphore_signal(barrier, inc=1, device_id=expert_at(here, z + 1), device_id_type=MESH)

    def greet(k, carry):
        there = lax.rem(here + k, g.plane)
        pl.semaphore_signal(barrier, inc=1, device_id=expert_at(there, z), device_id_type=MESH)
        return carry

    lax.fori_loop(1, g.plane, greet, 0)
    beside = jnp.where(z > 0, 1, 0) + jnp.where(z < last, 1, 0)
    pl.semaphore_wait(barrier, g.plane - 1 + beside)
    for copy in loads:
        copy.wait()

    def tok_copy(array, source, piece, way):
        rows = pl.ds(piece * g.chunk, g.chunk)
        ref = tok.at[array, source, rows]
        return pltpu.make_async_remote_copy(
            src_ref=ref,
            dst_ref=ref,
            send_sem=tok_send.at[way, array, source, piece],
            recv_sem=tok_recv.at[array, source, piece],
            device_id=expert_at(here, z + 1 - 2 * way),
            device_id_type=MESH,
        )

    def meta_copy(source, way):
        ref = meta.at[source]
        return pltpu.make_async_remote_copy(
            src_ref=ref,
            dst_ref=ref,
            send_sem=meta_send.at[way, source],
            recv_sem=meta_recv.at[source],
            device_id=expert_at(here, z + 1 - 2 * way),
            device_id_type=MESH,
        )

    def handed_on(step, make):
        for way in range(2):
            source = z - step if way == 0 else z + step
            inside = source >= 0 if way == 0 else source <= last
            onward = z < last if way == 0 else z > 0

            @pl.when(inside)
            def _():
                @pl.when(step > 0)
                def _():
                    make(source, way).wait_recv()

                @pl.when(onward)
                def _():
                    make(source, way).start()

    def gather_steps(arrays, first, stop):
        def one(step, carry):
            if 0 in arrays:
                handed_on(step, meta_copy)
            for piece in range(HALVES):
                for array in arrays:
                    handed_on(step, lambda source, way: tok_copy(array, source, piece, way))
            return carry

        lax.fori_loop(first, stop, one, 0)

    def make_picks(stream, group):
        base = base_of(group)
        low = lax.broadcasted_iota(jnp.int32, (2 * g.top, 2 * g.tokens), 1) < g.tokens
        pieces = []
        for pair in range(g.sources // 2):
            one, two = meta[base + 2 * pair], meta[base + 2 * pair + 1]
            if stream == 0:
                two = pltpu.roll(two, g.tokens, 1)
            else:
                one = pltpu.roll(one, g.tokens, 1)
            pieces.append(jnp.where(low, one, two))
        table = jnp.concatenate(pieces, axis=1) if len(pieces) > 1 else pieces[0]
        shape = (g.plane, g.group)
        expert = (lax.broadcasted_iota(jnp.int32, shape, 0) * g.line + z).astype(F32)
        chosen = jnp.zeros(shape, F32)
        gates = jnp.zeros(shape, F32)
        for k in range(g.top):
            hit = table[k : k + 1, :] == expert
            chosen = jnp.where(hit, 1.0, chosen)
            gates = jnp.where(hit, table[g.top + k : g.top + k + 1, :], gates)
        square = (g.group, g.group)
        above = lax.broadcasted_iota(jnp.int32, square, 0)
        right = lax.broadcasted_iota(jnp.int32, square, 1)
        earlier = (above < right) & (above // g.tokens == right // g.tokens)
        place = jnp.dot(
            chosen.astype(BF16), jnp.where(earlier, 1.0, 0.0).astype(BF16), preferred_element_type=F32
        )
        lane = lax.broadcasted_iota(jnp.int32, shape, 1) // g.tokens * g.capacity
        code = jnp.where(chosen > 0.0, lane.astype(F32) + place, -1.0)

        def spread(small):
            wide = jnp.broadcast_to(small[:, None, :], (g.plane, g.rows, g.group))
            return wide.reshape(g.group, g.group)

        slot = lax.rem(above, g.rows).astype(F32)
        hit = spread(code) == slot
        picks[stream, group] = jnp.where(hit, 1.0, 0.0).astype(BF16)
        by_row = jnp.where(hit, spread(gates), 0.0)
        if stream == 0:
            high = by_row.astype(BF16)
            weighted[group, 0] = high
            weighted[group, 1] = (by_row - high.astype(F32)).astype(BF16)
            return None
        return jnp.sum(by_row, axis=1, keepdims=True)

    def normed_rows(array, group):
        base = base_of(group)
        rows = tok[array, pl.ds(base, g.sources)].reshape(g.group, g.width).astype(F32)
        scale = lax.rsqrt(jnp.mean(rows * rows, axis=-1, keepdims=True) + EPSILON)
        return (rows * scale * gain_ref[...]).astype(BF16)

    def plane_copy(kind, group, source, target, there):
        slot = 2 * kind + group
        return pltpu.make_async_remote_copy(
            src_ref=source.at[pl.ds(there * g.rows, g.rows)],
            dst_ref=target.at[pl.ds(here * g.rows, g.rows)],
            send_sem=out_send.at[slot],
            recv_sem=out_recv.at[slot],
            device_id=expert_at(there, z),
            device_id_type=MESH,
        )

    def own_copy(kind, group, source, target):
        rows = pl.ds(here * g.rows, g.rows)
        return pltpu.make_async_copy(source.at[rows], target.at[rows], own_sem.at[2 * kind + group])

    def plane_send(kind, group, source, target):
        def one(k, carry):
            there = lax.rem(here + k, g.plane)
            plane_copy(kind, group, source, target, there).start()
            return carry

        lax.fori_loop(1, g.plane, one, 0)
        own_copy(kind, group, source, target).start()

    def all_but_one(kind, group, ref):
        most = ref.at[pl.ds(0, (g.plane - 1) * g.rows)]
        slot = 2 * kind + group
        return pltpu.make_async_remote_copy(
            src_ref=most,
            dst_ref=most,
            send_sem=out_send.at[slot],
            recv_sem=out_recv.at[slot],
            device_id=expert_at(lax.rem(here + 1, g.plane), z),
            device_id_type=MESH,
        )

    def plane_wait(kind, group, source, target):
        all_but_one(kind, group, target).wait_recv()
        own_copy(kind, group, source, target).wait()

    def dispatch_fwd(group):
        make_picks(0, group)
        rows = jnp.dot(picks[0, group], normed_rows(0, group), preferred_element_type=F32)
        send[0, group] = rows.astype(BF16)
        plane_send(0, group, send.at[0, group], recv.at[0, group])

    def dispatch_bwd(group):
        by_row = make_picks(1, group)
        rows = jnp.dot(picks[1, group], normed_rows(1, group), preferred_element_type=F32)
        send[1, group] = rows.astype(BF16)
        plane_send(1, group, send.at[1, group], recv.at[1, group])
        base = base_of(group)
        grads = tok[2, pl.ds(base, g.sources)].reshape(g.group, g.width)
        rows = jnp.dot(picks[1, group], grads, preferred_element_type=F32)
        send[2, group] = (rows * by_row).astype(BF16)
        plane_send(2, group, send.at[2, group], recv.at[2, group])

    def expert_fwd(group):
        plane_wait(0, group, send.at[0, group], recv.at[0, group])
        rows = recv[0, group]
        gate = jnp.dot(rows, w_gate[...], preferred_element_type=F32)
        upward = jnp.dot(rows, w_up[...], preferred_element_type=F32)
        hidden = (gate * jax.nn.sigmoid(gate) * upward).astype(BF16)
        made[0, group] = jnp.dot(hidden, w_down[...], preferred_element_type=F32).astype(BF16)
        plane_send(3, group, made.at[0, group], back.at[0, group])

    def expert_bwd(group):
        plane_wait(1, group, send.at[1, group], recv.at[1, group])
        rows = recv[1, group]
        gate = jnp.dot(rows, w_gate[...], preferred_element_type=F32)
        upward = jnp.dot(rows, w_up[...], preferred_element_type=F32)
        plane_wait(2, group, send.at[2, group], recv.at[2, group])
        d_hidden = transposed(recv[2, group], w_down[...])
        sigma = jax.nn.sigmoid(gate)
        d_gate = (d_hidden * upward * sigma * (1.0 + gate * (1.0 - sigma))).astype(BF16)
        d_up = (d_hidden * gate * sigma).astype(BF16)
        made[1, group] = (transposed(d_gate, w_gate[...]) + transposed(d_up, w_up[...])).astype(BF16)
        plane_send(4, group, made.at[1, group], back.at[1, group])

    def combine(stream, group):
        plane_wait(3 + stream, group, made.at[stream, group], back.at[stream, group])
        rows = back[stream, group]
        if stream == 0:
            total = picked_back(weighted[group, 0], rows) + picked_back(weighted[group, 1], rows)
        else:
            total = picked_back(picks[1, group], rows)
        part[stream, pl.ds(base_of(group), g.sources)] = total.reshape(g.sources, g.tokens, g.width)

    def sum_copy(stream, owner, piece, way):
        rows = pl.ds(piece * g.chunk, g.chunk)
        return pltpu.make_async_remote_copy(
            src_ref=stage.at[stream, owner, rows],
            dst_ref=acc.at[stream, way, owner, rows],
            send_sem=sum_send.at[stream, owner, piece],
            recv_sem=sum_recv.at[stream, way, owner, piece],
            device_id=expert_at(here, z + 1 - 2 * way),
            device_id_type=MESH,
        )

    def sum_steps(stream, first, stop):
        def one(step, carry):
            for piece in range(HALVES):
                rows = pl.ds(piece * g.chunk, g.chunk)
                for way in range(2):
                    owner = last - step if way == 0 else step
                    ahead = owner > z if way == 0 else owner < z
                    behind = z > 0 if way == 0 else z < last

                    @pl.when(ahead & behind)
                    def _():
                        sum_copy(stream, owner, piece, way).wait_recv()
                        total = part[stream, owner, rows] + acc[stream, way, owner, rows].astype(F32)
                        stage[stream, owner, rows] = total.astype(BF16)
                        sum_copy(stream, owner, piece, way).start()

                    @pl.when(ahead & jnp.logical_not(behind))
                    def _():
                        stage[stream, owner, rows] = part[stream, owner, rows].astype(BF16)
                        sum_copy(stream, owner, piece, way).start()

            return carry

        lax.fori_loop(first, stop, one, 0)

    def collected(stream):
        for way in range(2):
            behind = z > 0 if way == 0 else z < last

            @pl.when(behind)
            def _():
                for piece in range(HALVES):
                    sum_copy(stream, z, piece, way).wait_recv()
                part[stream, z] = part[stream, z] + acc[stream, way, z].astype(F32)

        return part[stream, z]

    def finish_fwd():
        y_ref[...] = (tok[0, z].astype(F32) + collected(0)).astype(BF16)

    def finish_bwd():
        summed = gain_ref[...] * collected(1)
        stream = tok[1, z].astype(F32)
        scale = lax.rsqrt(jnp.mean(stream * stream, axis=-1, keepdims=True) + EPSILON)
        inner = jnp.mean(summed * stream, axis=-1, keepdims=True)
        grad = tok[2, z].astype(F32)
        dx_ref[...] = (grad + scale * summed - stream * scale * scale * scale * inner).astype(BF16)

    near = g.sources
    gather_steps((0,), 0, near)
    gather_steps((1, 2), 0, 1)
    dispatch_fwd(0)
    gather_steps((0,), near, g.line)
    dispatch_fwd(1)
    gather_steps((1, 2), 1, 2)
    for copy in weights:
        copy.wait()
    expert_fwd(0)
    gather_steps((1, 2), 2, near)
    dispatch_bwd(0)
    gather_steps((1, 2), near, near + 1)
    expert_fwd(1)
    gather_steps((1, 2), near + 1, near + 2)
    combine(0, 0)
    gather_steps((1, 2), near + 2, near + 3)
    combine(0, 1)
    gather_steps((1, 2), near + 3, g.line)
    dispatch_bwd(1)
    sum_steps(0, 0, 2)
    expert_bwd(0)
    sum_steps(0, 2, 4)
    expert_bwd(1)
    sum_steps(0, 4, last)
    combine(1, 0)
    combine(1, 1)
    sum_steps(1, 0, last)
    finish_fwd()
    finish_bwd()

    for way in range(2):
        onward = z < last if way == 0 else z > 0

        @pl.when(onward)
        def _():
            def left(source, carry):
                sent = source <= z if way == 0 else source >= z

                @pl.when(sent)
                def _():
                    meta_copy(source, way).wait_send()
                    for array in range(3):
                        for piece in range(HALVES):
                            tok_copy(array, source, piece, way).wait_send()

                @pl.when(source > z if way == 0 else source < z)
                def _():
                    for stream in range(2):
                        for piece in range(HALVES):
                            sum_copy(stream, source, piece, way).wait_send()

                return carry

            lax.fori_loop(0, g.line, left, 0)

    for group in range(2):
        for kind in range(3):
            all_but_one(kind, group, send.at[kind, group]).wait_send()
        for stream in range(2):
            all_but_one(3 + stream, group, made.at[stream, group]).wait_send()


def passed_along(block, axis, distance):
    devices = range(lax.axis_size(axis))
    route = [((i - distance) % len(devices), i) for i in devices]
    return lax.ppermute(block, axis, route)


def on_device(
    line,
    fwd_input,
    fwd_routes,
    fwd_gates,
    bwd_input,
    bwd_grad,
    bwd_routes,
    bwd_gates,
    norm_gain,
    w_gate,
    w_up,
    w_down,
):
    _, tokens, width = fwd_input.shape
    top = fwd_routes.shape[2]
    hidden = w_gate.shape[3]
    g = geometry(lax.axis_size("expert"), tokens, top, width, hidden, line)
    routes = jnp.concatenate([fwd_routes[0], bwd_routes[0]], axis=0).astype(F32)
    gates = jnp.concatenate([fwd_gates[0], bwd_gates[0]], axis=0)
    meta = jnp.concatenate([routes, gates], axis=1).T
    block = jax.ShapeDtypeStruct((tokens, width), BF16)
    anywhere = pl.BlockSpec(memory_space=pl.ANY)
    in_vmem = pl.BlockSpec(memory_space=pltpu.VMEM)
    dma = pltpu.SemaphoreType.DMA
    y, dx = pl.pallas_call(
        functools.partial(kernel, g),
        out_shape=(block, block),
        in_specs=[anywhere, in_vmem] + [anywhere] * 6,
        out_specs=(in_vmem, in_vmem),
        scratch_shapes=[
            pltpu.VMEM((3, line, tokens, width), BF16),
            pltpu.VMEM((line, 2 * top, 2 * tokens), F32),
            pltpu.VMEM((width, hidden), BF16),
            pltpu.VMEM((width, hidden), BF16),
            pltpu.VMEM((hidden, width), BF16),
            pltpu.VMEM((2, 2, g.group, g.group), BF16),
            pltpu.VMEM((2, 2, g.group, g.group), BF16),
            pltpu.VMEM((3, 2, g.group, width), BF16),
            pltpu.VMEM((3, 2, g.group, width), BF16),
            pltpu.VMEM((2, 2, g.group, width), BF16),
            pltpu.VMEM((2, 2, g.group, width), BF16),
            pltpu.VMEM((2, line, tokens, width), F32),
            pltpu.VMEM((2, 2, line, tokens, width), BF16),
            pltpu.VMEM((2, line, tokens, width), BF16),
            dma((7,)),
            dma((2, 3, line, HALVES)),
            dma((3, line, HALVES)),
            dma((2, line)),
            dma((line,)),
            dma((10,)),
            dma((10,)),
            dma((10,)),
            dma((2, line, HALVES)),
            dma((2, 2, line, HALVES)),
        ],
        compiler_params=pltpu.CompilerParams(
            collective_id=0, has_side_effects=True, vmem_limit_bytes=56 * 1024 * 1024
        ),
        name="relay_tick",
    )(
        meta,
        norm_gain,
        fwd_input[0],
        bwd_input[0],
        bwd_grad[0],
        w_gate[0, 0],
        w_up[0, 0],
        w_down[0, 0],
    )
    return passed_along(y[None], "segment", 1), passed_along(dx[None], "segment", -1)


def solution(mesh, line=LINE):
    placed = (
        P("segment", "expert", None),
        P("segment", "expert", None),
        P("segment", "expert", None),
        P("segment", "expert", None),
        P("segment", "expert", None),
        P("segment", "expert", None),
        P("segment", "expert", None),
        P("segment", None),
        P("segment", "expert", None, None),
        P("segment", "expert", None, None),
        P("segment", "expert", None, None),
    )
    return jax.shard_map(
        functools.partial(on_device, line),
        mesh=mesh,
        in_specs=placed,
        out_specs=(P("segment", "expert", None), P("segment", "expert", None)),
        check_vma=False,
    )
```

```python
import functools
import types

import jax
import jax.numpy as jnp
from jax import lax
from jax.experimental import pallas as pl
from jax.experimental.pallas import tpu as pltpu
from jax.sharding import PartitionSpec as P

EPSILON = 1e-06
MESH = pl.DeviceIdType.MESH
F32 = jnp.float32
BF16 = jnp.bfloat16
LINE = 8
HALVES = 2
SCHEDULE = (
    ("gather", (0,), 0, 4),
    ("gather", (1, 2), 0, 1),
    ("dispatch_fwd", 0),
    ("gather", (0,), 4, 8),
    ("dispatch_fwd", 1),
    ("gather", (1, 2), 1, 2),
    ("weights",),
    ("expert_fwd", 0),
    ("gather", (1, 2), 2, 4),
    ("dispatch_bwd", 0),
    ("gather", (1, 2), 4, 5),
    ("expert_fwd", 1),
    ("gather", (1, 2), 5, 6),
    ("combine", 0, 0),
    ("gather", (1, 2), 6, 7),
    ("combine", 0, 1),
    ("gather", (1, 2), 7, 8),
    ("dispatch_bwd", 1),
    ("sum", 0, 0, 2),
    ("expert_bwd", 0),
    ("sum", 0, 2, 4),
    ("expert_bwd", 1),
    ("sum", 0, 4, 7),
    ("combine", 1, 0),
    ("combine", 1, 1),
    ("sum", 1, 0, 7),
    ("finish_fwd",),
    ("finish_bwd",),
)


def geometry(experts, tokens, top, width, hidden, line):
    g = types.SimpleNamespace()
    g.line = line
    g.plane = experts // line
    g.tokens = tokens
    g.top = top
    g.width = width
    g.hidden = hidden
    g.capacity = tokens * top // experts
    g.sources = line // 2
    g.rows = g.sources * g.capacity
    g.group = g.sources * tokens
    g.chunk = tokens // HALVES
    assert g.plane * g.rows == g.group
    return g


def transposed(left, right):
    return lax.dot_general(left, right, (((1,), (1,)), ((), ())), preferred_element_type=F32)


def picked_back(picks, rows):
    return lax.dot_general(picks, rows, (((0,), (0,)), ((), ())), preferred_element_type=F32)


def kernel(
    g,
    meta_in,
    gain_ref,
    fwd_in,
    bwd_in,
    grad_in,
    gate_hbm,
    up_hbm,
    down_hbm,
    y_ref,
    dx_ref,
    tok,
    meta,
    w_gate,
    w_up,
    w_down,
    picks,
    weighted,
    send,
    recv,
    made,
    back,
    part,
    acc,
    stage,
    load_sem,
    tok_send,
    tok_recv,
    meta_send,
    meta_recv,
    out_send,
    out_recv,
    own_sem,
    sum_send,
    sum_recv,
):
    me = lax.axis_index("expert")
    z = lax.rem(me, g.line)
    here = me // g.line
    half = z // g.sources
    last = g.line - 1

    def expert_at(plane, layer):
        return {"expert": plane * g.line + layer}

    def base_of(group):
        return lax.rem(half + group, 2) * g.sources

    loads = [
        pltpu.make_async_copy(meta_in, meta.at[z], load_sem.at[0]),
        pltpu.make_async_copy(fwd_in, tok.at[0, z], load_sem.at[1]),
        pltpu.make_async_copy(bwd_in, tok.at[1, z], load_sem.at[2]),
        pltpu.make_async_copy(grad_in, tok.at[2, z], load_sem.at[3]),
    ]
    weights = [
        pltpu.make_async_copy(gate_hbm, w_gate, load_sem.at[4]),
        pltpu.make_async_copy(up_hbm, w_up, load_sem.at[5]),
        pltpu.make_async_copy(down_hbm, w_down, load_sem.at[6]),
    ]
    for copy in loads + weights:
        copy.start()

    barrier = pltpu.get_barrier_semaphore()

    @pl.when(z > 0)
    def _():
        pl.semaphore_signal(barrier, inc=1, device_id=expert_at(here, z - 1), device_id_type=MESH)

    @pl.when(z < last)
    def _():
        pl.semaphore_signal(barrier, inc=1, device_id=expert_at(here, z + 1), device_id_type=MESH)

    def greet(k, carry):
        there = lax.rem(here + k, g.plane)
        pl.semaphore_signal(barrier, inc=1, device_id=expert_at(there, z), device_id_type=MESH)
        return carry

    lax.fori_loop(1, g.plane, greet, 0)
    beside = jnp.where(z > 0, 1, 0) + jnp.where(z < last, 1, 0)
    pl.semaphore_wait(barrier, g.plane - 1 + beside)
    for copy in loads:
        copy.wait()

    def tok_copy(array, source, piece, way):
        rows = pl.ds(piece * g.chunk, g.chunk)
        ref = tok.at[array, source, rows]
        return pltpu.make_async_remote_copy(
            src_ref=ref,
            dst_ref=ref,
            send_sem=tok_send.at[way, array, source, piece],
            recv_sem=tok_recv.at[array, source, piece],
            device_id=expert_at(here, z + 1 - 2 * way),
            device_id_type=MESH,
        )

    def meta_copy(source, way):
        ref = meta.at[source]
        return pltpu.make_async_remote_copy(
            src_ref=ref,
            dst_ref=ref,
            send_sem=meta_send.at[way, source],
            recv_sem=meta_recv.at[source],
            device_id=expert_at(here, z + 1 - 2 * way),
            device_id_type=MESH,
        )

    def handed_on(step, make):
        for way in range(2):
            source = z - step if way == 0 else z + step
            inside = source >= 0 if way == 0 else source <= last
            onward = z < last if way == 0 else z > 0

            @pl.when(inside)
            def _():
                @pl.when(step > 0)
                def _():
                    make(source, way).wait_recv()

                @pl.when(onward)
                def _():
                    make(source, way).start()

    def gather_steps(arrays, first, stop):
        def one(step, carry):
            if 0 in arrays:
                handed_on(step, meta_copy)
            for piece in range(HALVES):
                for array in arrays:
                    handed_on(step, lambda source, way: tok_copy(array, source, piece, way))
            return carry

        lax.fori_loop(first, stop, one, 0)

    def make_picks(stream, group):
        base = base_of(group)
        low = lax.broadcasted_iota(jnp.int32, (2 * g.top, 2 * g.tokens), 1) < g.tokens
        pieces = []
        for pair in range(g.sources // 2):
            one, two = meta[base + 2 * pair], meta[base + 2 * pair + 1]
            if stream == 0:
                two = pltpu.roll(two, g.tokens, 1)
            else:
                one = pltpu.roll(one, g.tokens, 1)
            pieces.append(jnp.where(low, one, two))
        table = jnp.concatenate(pieces, axis=1) if len(pieces) > 1 else pieces[0]
        shape = (g.plane, g.group)
        expert = (lax.broadcasted_iota(jnp.int32, shape, 0) * g.line + z).astype(F32)
        chosen = jnp.zeros(shape, F32)
        gates = jnp.zeros(shape, F32)
        for k in range(g.top):
            hit = table[k : k + 1, :] == expert
            chosen = jnp.where(hit, 1.0, chosen)
            gates = jnp.where(hit, table[g.top + k : g.top + k + 1, :], gates)
        square = (g.group, g.group)
        above = lax.broadcasted_iota(jnp.int32, square, 0)
        right = lax.broadcasted_iota(jnp.int32, square, 1)
        earlier = (above < right) & (above // g.tokens == right // g.tokens)
        place = jnp.dot(
            chosen.astype(BF16), jnp.where(earlier, 1.0, 0.0).astype(BF16), preferred_element_type=F32
        )
        lane = lax.broadcasted_iota(jnp.int32, shape, 1) // g.tokens * g.capacity
        code = jnp.where(chosen > 0.0, lane.astype(F32) + place, -1.0)

        def spread(small):
            wide = jnp.broadcast_to(small[:, None, :], (g.plane, g.rows, g.group))
            return wide.reshape(g.group, g.group)

        slot = lax.rem(above, g.rows).astype(F32)
        hit = spread(code) == slot
        picks[stream, group] = jnp.where(hit, 1.0, 0.0).astype(BF16)
        by_row = jnp.where(hit, spread(gates), 0.0)
        if stream == 0:
            high = by_row.astype(BF16)
            weighted[group, 0] = high
            weighted[group, 1] = (by_row - high.astype(F32)).astype(BF16)
            return None
        return jnp.sum(by_row, axis=1, keepdims=True)

    def normed_rows(array, group):
        base = base_of(group)
        rows = tok[array, pl.ds(base, g.sources)].reshape(g.group, g.width).astype(F32)
        scale = lax.rsqrt(jnp.mean(rows * rows, axis=-1, keepdims=True) + EPSILON)
        return (rows * scale * gain_ref[...]).astype(BF16)

    def plane_copy(kind, group, source, target, there):
        slot = 2 * kind + group
        return pltpu.make_async_remote_copy(
            src_ref=source.at[pl.ds(there * g.rows, g.rows)],
            dst_ref=target.at[pl.ds(here * g.rows, g.rows)],
            send_sem=out_send.at[slot],
            recv_sem=out_recv.at[slot],
            device_id=expert_at(there, z),
            device_id_type=MESH,
        )

    def own_copy(kind, group, source, target):
        rows = pl.ds(here * g.rows, g.rows)
        return pltpu.make_async_copy(source.at[rows], target.at[rows], own_sem.at[2 * kind + group])

    def plane_send(kind, group, source, target):
        def one(k, carry):
            there = lax.rem(here + k, g.plane)
            plane_copy(kind, group, source, target, there).start()
            return carry

        lax.fori_loop(1, g.plane, one, 0)
        own_copy(kind, group, source, target).start()

    def all_but_one(kind, group, ref):
        most = ref.at[pl.ds(0, (g.plane - 1) * g.rows)]
        slot = 2 * kind + group
        return pltpu.make_async_remote_copy(
            src_ref=most,
            dst_ref=most,
            send_sem=out_send.at[slot],
            recv_sem=out_recv.at[slot],
            device_id=expert_at(lax.rem(here + 1, g.plane), z),
            device_id_type=MESH,
        )

    def plane_wait(kind, group, source, target):
        all_but_one(kind, group, target).wait_recv()
        own_copy(kind, group, source, target).wait()

    def dispatch_fwd(group):
        make_picks(0, group)
        rows = jnp.dot(picks[0, group], normed_rows(0, group), preferred_element_type=F32)
        send[0, group] = rows.astype(BF16)
        plane_send(0, group, send.at[0, group], recv.at[0, group])

    def dispatch_bwd(group):
        by_row = make_picks(1, group)
        rows = jnp.dot(picks[1, group], normed_rows(1, group), preferred_element_type=F32)
        send[1, group] = rows.astype(BF16)
        plane_send(1, group, send.at[1, group], recv.at[1, group])
        base = base_of(group)
        grads = tok[2, pl.ds(base, g.sources)].reshape(g.group, g.width)
        rows = jnp.dot(picks[1, group], grads, preferred_element_type=F32)
        send[2, group] = (rows * by_row).astype(BF16)
        plane_send(2, group, send.at[2, group], recv.at[2, group])

    def expert_fwd(group):
        plane_wait(0, group, send.at[0, group], recv.at[0, group])
        rows = recv[0, group]
        gate = jnp.dot(rows, w_gate[...], preferred_element_type=F32)
        upward = jnp.dot(rows, w_up[...], preferred_element_type=F32)
        hidden = (gate * jax.nn.sigmoid(gate) * upward).astype(BF16)
        made[0, group] = jnp.dot(hidden, w_down[...], preferred_element_type=F32).astype(BF16)
        plane_send(3, group, made.at[0, group], back.at[0, group])

    def expert_bwd(group):
        plane_wait(1, group, send.at[1, group], recv.at[1, group])
        rows = recv[1, group]
        gate = jnp.dot(rows, w_gate[...], preferred_element_type=F32)
        upward = jnp.dot(rows, w_up[...], preferred_element_type=F32)
        plane_wait(2, group, send.at[2, group], recv.at[2, group])
        d_hidden = transposed(recv[2, group], w_down[...])
        sigma = jax.nn.sigmoid(gate)
        d_gate = (d_hidden * upward * sigma * (1.0 + gate * (1.0 - sigma))).astype(BF16)
        d_up = (d_hidden * gate * sigma).astype(BF16)
        made[1, group] = (transposed(d_gate, w_gate[...]) + transposed(d_up, w_up[...])).astype(BF16)
        plane_send(4, group, made.at[1, group], back.at[1, group])

    def combine(stream, group):
        plane_wait(3 + stream, group, made.at[stream, group], back.at[stream, group])
        rows = back[stream, group]
        if stream == 0:
            total = picked_back(weighted[group, 0], rows) + picked_back(weighted[group, 1], rows)
        else:
            total = picked_back(picks[1, group], rows)
        part[stream, pl.ds(base_of(group), g.sources)] = total.reshape(g.sources, g.tokens, g.width)

    def sum_copy(stream, owner, piece, way):
        rows = pl.ds(piece * g.chunk, g.chunk)
        return pltpu.make_async_remote_copy(
            src_ref=stage.at[stream, owner, rows],
            dst_ref=acc.at[stream, way, owner, rows],
            send_sem=sum_send.at[stream, owner, piece],
            recv_sem=sum_recv.at[stream, way, owner, piece],
            device_id=expert_at(here, z + 1 - 2 * way),
            device_id_type=MESH,
        )

    def sum_steps(stream, first, stop):
        def one(step, carry):
            for piece in range(HALVES):
                rows = pl.ds(piece * g.chunk, g.chunk)
                for way in range(2):
                    from_end = z if way == 0 else last - z
                    owner = last - (step - from_end) if way == 0 else step - from_end

                    @pl.when((step >= from_end) & (from_end > 0))
                    def _():
                        sum_copy(stream, owner, piece, way).wait_recv()
                        total = part[stream, owner, rows] + acc[stream, way, owner, rows].astype(F32)
                        stage[stream, owner, rows] = total.astype(BF16)
                        sum_copy(stream, owner, piece, way).start()

                    @pl.when(from_end == 0)
                    def _():
                        stage[stream, owner, rows] = part[stream, owner, rows].astype(BF16)
                        sum_copy(stream, owner, piece, way).start()

            return carry

        lax.fori_loop(first, stop, one, 0)

    def collected(stream):
        for way in range(2):
            behind = z > 0 if way == 0 else z < last

            @pl.when(behind)
            def _():
                for piece in range(HALVES):
                    sum_copy(stream, z, piece, way).wait_recv()
                part[stream, z] = part[stream, z] + acc[stream, way, z].astype(F32)

        return part[stream, z]

    def finish_fwd():
        y_ref[...] = (tok[0, z].astype(F32) + collected(0)).astype(BF16)

    def finish_bwd():
        summed = gain_ref[...] * collected(1)
        stream = tok[1, z].astype(F32)
        scale = lax.rsqrt(jnp.mean(stream * stream, axis=-1, keepdims=True) + EPSILON)
        inner = jnp.mean(summed * stream, axis=-1, keepdims=True)
        grad = tok[2, z].astype(F32)
        dx_ref[...] = (grad + scale * summed - stream * scale * scale * scale * inner).astype(BF16)

    do = {
        "gather": gather_steps,
        "sum": sum_steps,
        "dispatch_fwd": dispatch_fwd,
        "dispatch_bwd": dispatch_bwd,
        "expert_fwd": expert_fwd,
        "expert_bwd": expert_bwd,
        "combine": combine,
        "finish_fwd": finish_fwd,
        "finish_bwd": finish_bwd,
    }
    for name, *rest in SCHEDULE:
        if name == "weights":
            for copy in weights:
                copy.wait()
        else:
            do[name](*rest)

    names = [entry[0] for entry in SCHEDULE]
    arrays = sorted({array for entry in SCHEDULE if entry[0] == "gather" for array in entry[1]})
    streams = sorted({entry[1] for entry in SCHEDULE if entry[0] == "sum"})
    for way in range(2):
        onward = z < last if way == 0 else z > 0

        @pl.when(onward)
        def _():
            def left(source, carry):
                sent = source <= z if way == 0 else source >= z

                @pl.when(sent)
                def _():
                    if 0 in arrays:
                        meta_copy(source, way).wait_send()
                    for array in arrays:
                        for piece in range(HALVES):
                            tok_copy(array, source, piece, way).wait_send()

                @pl.when(source > z if way == 0 else source < z)
                def _():
                    for stream in streams:
                        for piece in range(HALVES):
                            sum_copy(stream, source, piece, way).wait_send()

                return carry

            lax.fori_loop(0, g.line, left, 0)

    for name, *rest in SCHEDULE:
        if name == "dispatch_fwd":
            all_but_one(0, rest[0], send.at[0, rest[0]]).wait_send()
        if name == "dispatch_bwd":
            all_but_one(1, rest[0], send.at[1, rest[0]]).wait_send()
            all_but_one(2, rest[0], send.at[2, rest[0]]).wait_send()
        if name == "expert_fwd":
            all_but_one(3, rest[0], made.at[0, rest[0]]).wait_send()
        if name == "expert_bwd":
            all_but_one(4, rest[0], made.at[1, rest[0]]).wait_send()


def passed_along(block, axis, distance):
    devices = range(lax.axis_size(axis))
    route = [((i - distance) % len(devices), i) for i in devices]
    return lax.ppermute(block, axis, route)


def on_device(
    line,
    fwd_input,
    fwd_routes,
    fwd_gates,
    bwd_input,
    bwd_grad,
    bwd_routes,
    bwd_gates,
    norm_gain,
    w_gate,
    w_up,
    w_down,
):
    _, tokens, width = fwd_input.shape
    top = fwd_routes.shape[2]
    hidden = w_gate.shape[3]
    g = geometry(lax.axis_size("expert"), tokens, top, width, hidden, line)
    routes = jnp.concatenate([fwd_routes[0], bwd_routes[0]], axis=0).astype(F32)
    gates = jnp.concatenate([fwd_gates[0], bwd_gates[0]], axis=0)
    meta = jnp.concatenate([routes, gates], axis=1).T
    block = jax.ShapeDtypeStruct((tokens, width), BF16)
    anywhere = pl.BlockSpec(memory_space=pl.ANY)
    in_vmem = pl.BlockSpec(memory_space=pltpu.VMEM)
    dma = pltpu.SemaphoreType.DMA
    y, dx = pl.pallas_call(
        functools.partial(kernel, g),
        out_shape=(block, block),
        in_specs=[anywhere, in_vmem] + [anywhere] * 6,
        out_specs=(in_vmem, in_vmem),
        scratch_shapes=[
            pltpu.VMEM((3, line, tokens, width), BF16),
            pltpu.VMEM((line, 2 * top, 2 * tokens), F32),
            pltpu.VMEM((width, hidden), BF16),
            pltpu.VMEM((width, hidden), BF16),
            pltpu.VMEM((hidden, width), BF16),
            pltpu.VMEM((2, 2, g.group, g.group), BF16),
            pltpu.VMEM((2, 2, g.group, g.group), BF16),
            pltpu.VMEM((3, 2, g.group, width), BF16),
            pltpu.VMEM((3, 2, g.group, width), BF16),
            pltpu.VMEM((2, 2, g.group, width), BF16),
            pltpu.VMEM((2, 2, g.group, width), BF16),
            pltpu.VMEM((2, line, tokens, width), F32),
            pltpu.VMEM((2, 2, line, tokens, width), BF16),
            pltpu.VMEM((2, line, tokens, width), BF16),
            dma((7,)),
            dma((2, 3, line, HALVES)),
            dma((3, line, HALVES)),
            dma((2, line)),
            dma((line,)),
            dma((10,)),
            dma((10,)),
            dma((10,)),
            dma((2, line, HALVES)),
            dma((2, 2, line, HALVES)),
        ],
        compiler_params=pltpu.CompilerParams(
            collective_id=0, has_side_effects=True, vmem_limit_bytes=56 * 1024 * 1024
        ),
        name="relay_tick",
    )(
        meta,
        norm_gain,
        fwd_input[0],
        bwd_input[0],
        bwd_grad[0],
        w_gate[0, 0],
        w_up[0, 0],
        w_down[0, 0],
    )
    return passed_along(y[None], "segment", 1), passed_along(dx[None], "segment", -1)


def solution(mesh, line=LINE):
    placed = (
        P("segment", "expert", None),
        P("segment", "expert", None),
        P("segment", "expert", None),
        P("segment", "expert", None),
        P("segment", "expert", None),
        P("segment", "expert", None),
        P("segment", "expert", None),
        P("segment", None),
        P("segment", "expert", None, None),
        P("segment", "expert", None, None),
        P("segment", "expert", None, None),
    )
    return jax.shard_map(
        functools.partial(on_device, line),
        mesh=mesh,
        in_specs=placed,
        out_specs=(P("segment", "expert", None), P("segment", "expert", None)),
        check_vma=False,
    )
```
